32 devices in a mesh: group: 8 (over y, x, core), rep: 4 (over z).
Axes of the slice: x: 2, y: 2, z: 4, core: 2. Of those that a mesh axis runs over, the one named last changes fastest.
Arguments:
- tokens: bfloat16 [8192, 768], P(('group', 'rep')), may hold values from -6 to 6
- segments: int32 [8192], P(('group', 'rep')), may hold values from -1 to 3, as said below
- attn_in_weight: bfloat16 [2, 768, 2304], P(None, 'group'), may hold values from -8 to 8
- attn_bias: bfloat16 [2, 3, 768], P(None, None, 'group'), may hold values from -1.75 to 1.75
- out_weight: bfloat16 [2, 768, 768], P(None, 'group'), may hold values from -0.875 to 0.875
- fc1_weight: bfloat16 [2, 768, 3072], P(None, 'group'), may hold values from -0.21875 to 0.21875
- fc1_bias: bfloat16 [2, 3072], P(None, 'group'), may hold values from -1.75 to 1.75
- fc2_weight: bfloat16 [2, 3072, 768], P(None, 'group'), may hold values from -0.109375 to 0.109375
- fc2_bias: bfloat16 [2, 768], P(None, 'group'), may hold values from -1.75 to 1.75
- ln_gain: bfloat16 [2, 2, 768], P(None, None, 'group'), may hold values from 0.25 to 1.75
- ln_bias: bfloat16 [2, 2, 768], P(None, None, 'group'), may hold values from -1.75 to 1.75
- cotangent: bfloat16 [8192, 768], P(('group', 'rep')), may hold values from -12 to 12
Outputs:
- output: float32 [8192, 768], P(('group', 'rep'))
- input_grad: float32 [8192, 768], P(('group', 'rep'))
- grad_attn_in: float32 [2, 768, 2304], P(None, 'group')
- grad_attn_bias: float32 [2, 3, 768], P(None, None, 'group')
- grad_out_weight: float32 [2, 768, 768], P(None, 'group')
- grad_fc1_weight: float32 [2, 768, 3072], P(None, 'group')
- grad_fc1_bias: float32 [2, 3072], P(None, 'group')
- grad_fc2_weight: float32 [2, 3072, 768], P(None, 'group')
- grad_fc2_bias: float32 [2, 768], P(None, 'group')
- grad_ln_gain: float32 [2, 2, 768], P(None, None, 'group')
- grad_ln_bias: float32 [2, 2, 768], P(None, None, 'group')
The draws below stay inside these ranges and needn't reach their ends.
Inputs may be any that keep to these rules, and one draw needn't show every extreme that they name: `segments`: each clip occupies exactly 1500 consecutive positions, clip numbers rise by one along the tokens, the first clip starts at the first token, padding elsewhere.
All inputs are finite; a program needn't handle non-finite values.
Results may differ from the reference program's by a relative error of at most 0.017.
Values may be sent and summed in bfloat16 or wider, within the bound.
No kernel may reach another device: no remote copies, remote signals or barrier semaphores. Data moves between devices by JAX's collectives and lax.ppermute only.
A program may use at most 256 MiB of HBM per device.

```python
import math
import jax
import jax.numpy as jnp
from jax import lax

D = 768
H = 12
HD = 64
FF = 3072
MAXLEN = 1500
LAYERS = 2
TOKENS = 8192
CLIPS = 4


def draw_segments(key, part):
    spare = TOKENS - CLIPS * MAXLEN
    weights = jax.random.randint(key, (CLIPS + 1,), 1, 100, jnp.int32)
    weights = jnp.where(jnp.arange(CLIPS + 1, dtype=jnp.int32) == 0, 0, weights)
    running = jnp.cumsum(weights)
    overall = running[CLIPS]
    before = spare * running[:CLIPS] // overall
    starts = jnp.arange(CLIPS, dtype=jnp.int32) * MAXLEN + before
    places = jnp.arange(TOKENS, dtype=jnp.int32)
    inside = (places[:, None] >= starts[None, :]) & (places[:, None] < starts[None, :] + MAXLEN)
    numbers = jnp.arange(CLIPS, dtype=jnp.int32) + 1
    return jnp.sum(jnp.where(inside, numbers[None, :], 0), axis=1).astype(jnp.int32) - 1


def draw_attn_in_weight(key, part):
    first_key = jax.random.fold_in(key, 11)
    base = jax.random.normal(first_key, (LAYERS, D, 3 * D), jnp.float32) * D ** (-0.5)
    return base.astype(jnp.bfloat16)


def strengthened(values, own_key, source, target, shards_of, factor):
    owner, partner = [(jnp.arange(values.shape[axis_at]) // (values.shape[axis_at] // shards_of)).reshape([-1 if axis == axis_at else 1 for axis in range(values.ndim)]) for axis_at in (source, target)]
    chosen = jax.random.permutation(own_key, shards_of)[partner]
    strong = (owner == chosen) | (owner == (partner + shards_of // 2) % shards_of)
    return jnp.where(strong, factor * values, values)


def levels(own_key, shape, pieces, low, high):
    def one(axis_at, blocks):
        steps = jax.random.uniform(jax.random.fold_in(jax.random.fold_in(own_key, 6), axis_at), (blocks,), jnp.float32, low / len(pieces), high / len(pieces))
        return jnp.repeat(jnp.exp(steps), shape[axis_at] // blocks).reshape((-1,) + (1,) * (len(shape) - axis_at - 1))

    level = one(*pieces[0])
    for cut in pieces[1:]:
        level = level * one(*cut)
    return level


def noise(own_key, shape, scale, bound, cuts=(), kind=jnp.bfloat16):
    level = levels(own_key, shape, cuts, -0.22, 0.18) if cuts else 1.0
    values = jax.random.normal(own_key, shape, jnp.float32) * scale * level
    return jnp.minimum(jnp.maximum(values, -bound), bound).astype(kind)


def noise_with(rng, shape, scale, reach, cuts, heavy, kind=jnp.bfloat16):
    values = scale * jax.random.normal(rng, shape, jnp.float32)
    if cuts:
        values = values * levels(rng, shape, cuts, -0.22, 0.18)
    return jnp.clip(strengthened(values, jax.random.fold_in(rng, 3), *heavy), -reach, reach).astype(kind)


def setup_inputs(seed: int = 0) -> dict:
    streams_of = jax.random.split(jax.random.key(seed), 13)
    return {
        "tokens": noise(streams_of[0], (TOKENS, D), 1.0, 6.0, ((0, 32),)),
        "segments": draw_segments(jax.random.fold_in(streams_of[12], 71), 0),
        "attn_in_weight": draw_attn_in_weight(jax.random.fold_in(streams_of[12], 71), 0),
        "attn_bias": noise(streams_of[3], (LAYERS, 3, D), 0.3, 1.75, ((2, 8),)),
        "out_weight": noise(streams_of[4], (LAYERS, D, D), (D // 16) ** -0.5, 0.875, ((1, 8),)),
        "fc1_weight": noise(streams_of[5], (LAYERS, D, FF), D ** -0.5, 0.21875, ((1, 8),)),
        "fc1_bias": noise(streams_of[6], (LAYERS, FF), 0.3, 1.75, ((1, 8),)),
        "fc2_weight": noise(streams_of[7], (LAYERS, FF, D), FF ** -0.5, 0.109375, ((1, 8),)),
        "fc2_bias": noise(streams_of[8], (LAYERS, D), 0.3, 1.75, ((1, 8),)),
        "ln_gain": jnp.clip(1.0 + 0.15 * jax.random.normal(streams_of[9], (LAYERS, 2, D), jnp.float32), 0.25, 1.75).astype(jnp.bfloat16),
        "ln_bias": noise(streams_of[10], (LAYERS, 2, D), 0.3, 1.75, ((2, 8),)),
        "cotangent": noise_with(streams_of[11], (TOKENS, D), 1.0, 12.0, ((0, 32),), (0, 1, 32, 2.75)),
    }


EPSILON = 1e-05

def layer_norm(values, gain, offset):
    center = lax.optimization_barrier(jnp.mean(values, axis=-1, keepdims=True))
    shifted = values - center
    spread = lax.optimization_barrier(jnp.mean(shifted * shifted, axis=-1, keepdims=True))
    inverse = lax.rsqrt(spread + EPSILON)
    unit_rows = shifted * inverse
    return (unit_rows * gain.astype(jnp.float32) + offset.astype(jnp.float32), unit_rows, inverse)

def norm_back(upstream, unit_rows, inverse, gain):
    scaled = upstream * gain.astype(jnp.float32)
    result = inverse * (scaled - lax.optimization_barrier(jnp.mean(scaled, axis=-1, keepdims=True)) - unit_rows * lax.optimization_barrier(jnp.mean(scaled * unit_rows, axis=-1, keepdims=True)))
    return (result, lax.optimization_barrier(jnp.sum(upstream * unit_rows, axis=0)), lax.optimization_barrier(jnp.sum(upstream, axis=0)))

def gelu_slope(inputs):
    normal_cdf = 0.5 * (1.0 + lax.erf(inputs * 0.7071067811865476))
    return normal_cdf + inputs * jnp.exp(-0.5 * inputs * inputs) * 0.3989422804014327

def block_mask(query_labels, key_labels, block_rows):
    query_place = lax.iota(jnp.int32, block_rows) + MAXLEN
    key_place = lax.iota(jnp.int32, key_labels.shape[0])
    same = query_labels[:, None] == key_labels[None, :]
    return same & ((query_labels[:, None] >= 2) | (query_place[:, None] == key_place[None, :]))

def padded_inputs(key_rows, value_rows, labels):
    key_pad = jnp.pad(key_rows, ((MAXLEN, MAXLEN), (0, 0)))
    value_pad = jnp.pad(value_rows, ((MAXLEN, MAXLEN), (0, 0)))
    label_pad = jnp.pad(labels, (MAXLEN, MAXLEN))
    return (key_pad, value_pad, label_pad)

def attention_forward(queries, key_rows, value_rows, labels):
    block_rows = math.gcd(TOKENS, 4096)
    window_span = block_rows + 2 * MAXLEN
    key_pad, value_pad, label_pad = padded_inputs(key_rows, value_rows, labels)

    def one_block(block_at):
        start = block_at * block_rows
        query_block = lax.dynamic_slice_in_dim(queries, start, block_rows, 0)
        key_block = lax.dynamic_slice_in_dim(key_pad, start, window_span, 0)
        value_block = lax.dynamic_slice_in_dim(value_pad, start, window_span, 0)
        allowed = block_mask(lax.dynamic_slice_in_dim(labels, start, block_rows, 0), lax.dynamic_slice_in_dim(label_pad, start, window_span, 0), block_rows)

        def one_head(head_at):
            offset = head_at * HD
            query_head = lax.dynamic_slice_in_dim(query_block, offset, HD, 1)
            key_head = lax.dynamic_slice_in_dim(key_block, offset, HD, 1)
            value_head = lax.dynamic_slice_in_dim(value_block, offset, HD, 1)
            scores = jnp.dot(query_head, key_head.T, preferred_element_type=jnp.float32)
            scores = jnp.where(allowed, scores, -1e+30)
            top_score = lax.optimization_barrier(jnp.max(scores, axis=1, keepdims=True))
            expd = jnp.exp(scores - top_score)
            total = lax.optimization_barrier(jnp.sum(expd, axis=1, keepdims=True))
            probs = (expd / total).astype(jnp.bfloat16)
            heard = jnp.dot(probs, value_head, preferred_element_type=jnp.float32)
            return (heard, top_score[:, 0] + jnp.log(total[:, 0]))
        heads_out, heads_lse = lax.map(one_head, jnp.arange(H, dtype=jnp.int32))
        return (heads_out.transpose(1, 0, 2).reshape(block_rows, H * HD), heads_lse.T)
    outputs, log_totals = lax.map(one_block, jnp.arange(TOKENS // block_rows, dtype=jnp.int32))
    return (outputs.reshape(TOKENS, H * HD), log_totals.reshape(TOKENS, H))

def attention_backward(queries, key_rows, value_rows, labels, log_totals, upstream):
    block_rows = math.gcd(TOKENS, 4096)
    window_span = block_rows + 2 * MAXLEN
    key_pad, value_pad, label_pad = padded_inputs(key_rows, value_rows, labels)

    def one_block(carried, block_at):
        d_key_pad, d_value_pad = carried
        start = block_at * block_rows
        query_block = lax.dynamic_slice_in_dim(queries, start, block_rows, 0)
        key_block = lax.dynamic_slice_in_dim(key_pad, start, window_span, 0)
        value_block = lax.dynamic_slice_in_dim(value_pad, start, window_span, 0)
        total_block = lax.dynamic_slice_in_dim(log_totals, start, block_rows, 0)
        upstream_block = lax.dynamic_slice_in_dim(upstream, start, block_rows, 0)
        allowed = block_mask(lax.dynamic_slice_in_dim(labels, start, block_rows, 0), lax.dynamic_slice_in_dim(label_pad, start, window_span, 0), block_rows)

        def one_head(head_at):
            offset = head_at * HD
            query_head = lax.dynamic_slice_in_dim(query_block, offset, HD, 1)
            key_head = lax.dynamic_slice_in_dim(key_block, offset, HD, 1)
            value_head = lax.dynamic_slice_in_dim(value_block, offset, HD, 1)
            upstream_head = lax.dynamic_slice_in_dim(upstream_block, offset, HD, 1)
            total_head = lax.dynamic_slice_in_dim(total_block, head_at, 1, 1)[:, 0]
            scores = jnp.dot(query_head, key_head.T, preferred_element_type=jnp.float32)
            probs = jnp.where(allowed, jnp.exp(scores - total_head[:, None]), 0.0)
            rounded = probs.astype(jnp.bfloat16)
            d_value = jnp.dot(rounded.T, upstream_head, preferred_element_type=jnp.float32)
            d_probs = jnp.dot(upstream_head, value_head.T, preferred_element_type=jnp.float32)
            delta = lax.optimization_barrier(jnp.sum(probs * d_probs, axis=1, keepdims=True))
            d_scores = (probs * (d_probs - delta)).astype(jnp.bfloat16)
            d_query = jnp.dot(d_scores, key_head, preferred_element_type=jnp.float32)
            d_key = jnp.dot(d_scores.T, query_head, preferred_element_type=jnp.float32)
            return (d_query, d_key, d_value)
        d_query, d_key, d_value = lax.map(one_head, jnp.arange(H, dtype=jnp.int32))
        d_key = d_key.transpose(1, 0, 2).reshape(window_span, H * HD)
        d_value = d_value.transpose(1, 0, 2).reshape(window_span, H * HD)
        d_key_pad = lax.dynamic_update_slice_in_dim(d_key_pad, lax.dynamic_slice_in_dim(d_key_pad, start, window_span, 0) + d_key, start, 0)
        d_value_pad = lax.dynamic_update_slice_in_dim(d_value_pad, lax.dynamic_slice_in_dim(d_value_pad, start, window_span, 0) + d_value, start, 0)
        return ((d_key_pad, d_value_pad), d_query.transpose(1, 0, 2).reshape(block_rows, H * HD))
    zero_pad = jnp.zeros((TOKENS + 2 * MAXLEN, H * HD), jnp.float32)
    (d_key_pad, d_value_pad), d_queries = lax.scan(one_block, (zero_pad, zero_pad), jnp.arange(TOKENS // block_rows, dtype=jnp.int32))
    return (d_queries.reshape(TOKENS, H * HD), d_key_pad[MAXLEN:MAXLEN + TOKENS], d_value_pad[MAXLEN:MAXLEN + TOKENS])

def forward_layer(resid, labels, weights):
    w_in, b_attn, w_out, w_up, b_up, w_down, b_down, gains, offsets = weights
    width = H * HD
    normed, unit_first, inverse_first = layer_norm(resid, gains[0], offsets[0])
    first = normed.astype(jnp.bfloat16)
    mixed = jnp.dot(first, w_in, preferred_element_type=jnp.float32)
    queries = ((mixed[:, :width] + b_attn[0].astype(jnp.float32)) * HD ** (-0.5)).astype(jnp.bfloat16)
    key_rows = mixed[:, width:2 * width].astype(jnp.bfloat16)
    value_rows = (mixed[:, 2 * width:] + b_attn[1].astype(jnp.float32)).astype(jnp.bfloat16)
    attended, log_totals = attention_forward(queries, key_rows, value_rows, labels)
    heard = attended.astype(jnp.bfloat16)
    middle = resid + jnp.dot(heard, w_out, preferred_element_type=jnp.float32) + b_attn[2].astype(jnp.float32)
    normed_two, unit_second, inverse_second = layer_norm(middle, gains[1], offsets[1])
    second = normed_two.astype(jnp.bfloat16)
    pre_act = jnp.dot(second, w_up, preferred_element_type=jnp.float32) + b_up.astype(jnp.float32)
    active = jax.nn.gelu(pre_act, approximate=False).astype(jnp.bfloat16)
    result = middle + jnp.dot(active, w_down, preferred_element_type=jnp.float32) + b_down.astype(jnp.float32)
    stored = (unit_first, inverse_first, first, queries, key_rows, value_rows, heard, log_totals, unit_second, inverse_second, second, pre_act, active)
    return (result, stored)

def backward_layer(upstream, labels, weights, stored):
    w_in, b_attn, w_out, w_up, b_up, w_down, b_down, gains, offsets = weights
    unit_first, inverse_first, first, queries, key_rows, value_rows, heard, log_totals, unit_second, inverse_second, second, pre_act, active = stored
    down_rounded = upstream.astype(jnp.bfloat16)
    g_down_b = lax.optimization_barrier(jnp.sum(upstream, axis=0))
    g_down_w = jnp.dot(active.T, down_rounded, preferred_element_type=jnp.float32)
    d_pre = jnp.dot(down_rounded, w_down.T, preferred_element_type=jnp.float32) * gelu_slope(pre_act)
    up_rounded = d_pre.astype(jnp.bfloat16)
    g_up_b = lax.optimization_barrier(jnp.sum(d_pre, axis=0))
    g_up_w = jnp.dot(second.T, up_rounded, preferred_element_type=jnp.float32)
    d_second = jnp.dot(up_rounded, w_up.T, preferred_element_type=jnp.float32)
    d_norm_two, g_gain_two, g_offset_two = norm_back(d_second, unit_second, inverse_second, gains[1])
    d_middle = upstream + d_norm_two
    middle_rounded = d_middle.astype(jnp.bfloat16)
    g_out_b = lax.optimization_barrier(jnp.sum(d_middle, axis=0))
    g_out_w = jnp.dot(heard.T, middle_rounded, preferred_element_type=jnp.float32)
    d_heard = jnp.dot(middle_rounded, w_out.T, preferred_element_type=jnp.float32).astype(jnp.bfloat16)
    d_queries, d_keys, d_values = attention_backward(queries, key_rows, value_rows, labels, log_totals, d_heard)
    d_queries = d_queries * HD ** (-0.5)
    d_mixed = jnp.concatenate([d_queries, d_keys, d_values], axis=1)
    mixed_rounded = d_mixed.astype(jnp.bfloat16)
    g_attn_b = jnp.stack([lax.optimization_barrier(jnp.sum(d_queries, axis=0)), lax.optimization_barrier(jnp.sum(d_values, axis=0)), g_out_b])
    g_in_w = jnp.dot(first.T, mixed_rounded, preferred_element_type=jnp.float32)
    d_first = jnp.dot(mixed_rounded, w_in.T, preferred_element_type=jnp.float32)
    d_norm_one, g_gain_one, g_offset_one = norm_back(d_first, unit_first, inverse_first, gains[0])
    d_resid = d_middle + d_norm_one
    grads = (g_in_w, g_attn_b, g_out_w, g_up_w, g_up_b, g_down_w, g_down_b, jnp.stack([g_gain_one, g_gain_two]), jnp.stack([g_offset_one, g_offset_two]))
    return (d_resid, grads)

def reference(tokens, segments, attn_in_weight, attn_bias, out_weight, fc1_weight, fc1_bias, fc2_weight, fc2_bias, ln_gain, ln_bias, cotangent):
    labels = segments + 2
    resid = tokens.astype(jnp.float32)
    every_weight = []
    every_store = []
    for layer_at in range(LAYERS):
        weights = (attn_in_weight[layer_at], attn_bias[layer_at], out_weight[layer_at], fc1_weight[layer_at], fc1_bias[layer_at], fc2_weight[layer_at], fc2_bias[layer_at], ln_gain[layer_at], ln_bias[layer_at])
        resid, stored = forward_layer(resid, labels, weights)
        every_weight.append(weights)
        every_store.append(stored)
    upstream = cotangent.astype(jnp.float32)
    layer_grads = [None] * LAYERS
    for layer_at in reversed(range(LAYERS)):
        upstream, grads = backward_layer(upstream, labels, every_weight[layer_at], every_store[layer_at])
        layer_grads[layer_at] = grads
    stacked = [jnp.stack([layer_grads[layer_at][field] for layer_at in range(LAYERS)]) for field in range(9)]
    return (resid, upstream, stacked[0], stacked[1], stacked[2], stacked[3], stacked[4], stacked[5], stacked[6], stacked[7], stacked[8])
```

```python
import functools

import jax
import jax.numpy as jnp
from jax import lax
from jax.experimental import pallas as pl
from jax.experimental.pallas import tpu as pltpu
from jax.sharding import PartitionSpec as P

H = 12
HD = 64
LAYERS = 2
MAXLEN = 1500
SPLIT = 4
HEADS = H // SPLIT
WIDE = HEADS * HD
QROWS = 256
KROWS = 512
EPSILON = 1e-05
AXES = ("group", "rep")
NT = (((1,), (1,)), ((), ()))
NN = (((1,), (0,)), ((), ()))
TN = (((0,), (0,)), ((), ()))


def dot32(a, b, dims):
    return lax.dot_general(a, b, dims, preferred_element_type=jnp.float32)


def layer_norm(values, gain, offset):
    center = jnp.mean(values, axis=-1, keepdims=True)
    shifted = values - center
    spread = jnp.mean(shifted * shifted, axis=-1, keepdims=True)
    inverse = lax.rsqrt(spread + EPSILON)
    unit_rows = shifted * inverse
    return (unit_rows * gain + offset, unit_rows, inverse)


def norm_back(upstream, unit_rows, inverse, gain):
    scaled = upstream * gain
    result = inverse * (
        scaled
        - jnp.mean(scaled, axis=-1, keepdims=True)
        - unit_rows * jnp.mean(scaled * unit_rows, axis=-1, keepdims=True)
    )
    return (result, jnp.sum(upstream * unit_rows, axis=0), jnp.sum(upstream, axis=0))


def gelu_slope(inputs):
    normal_cdf = 0.5 * (1.0 + lax.erf(inputs * 0.7071067811865476))
    return normal_cdf + inputs * jnp.exp(-0.5 * inputs * inputs) * 0.3989422804014327


def head_rows(rows):
    lane = lax.broadcasted_iota(jnp.int32, (rows.shape[0], 2 * HD), 1)
    pair = rows[:, : 2 * HD]
    zero = jnp.zeros_like(pair)
    first = jnp.where(lane < HD, pair, zero)
    second = jnp.where(lane >= HD, pair, zero)
    last = jnp.concatenate([rows[:, 2 * HD :], jnp.zeros((rows.shape[0], HD), rows.dtype)], axis=1)
    return first, second, last


def head_rows_up(rows):
    first, second, _ = head_rows(rows)
    last = jnp.concatenate([jnp.zeros((rows.shape[0], HD), rows.dtype), rows[:, 2 * HD :]], axis=1)
    return first, second, last


KEY_TILE = (0, 0, 1)
VALUE_TILE = (2, 2, 1)


def attend_kernel(bounds, q_ref, kv_ref, low_ref, high_ref, o_ref, lse_ref, top, total, acc):
    block = pl.program_id(0)
    rows = q_ref.shape[0]
    queries = head_rows(q_ref[...])
    low = low_ref[...]
    high = high_ref[...]
    top[...] = jnp.full(top.shape, -1e30, jnp.float32)
    total[...] = jnp.zeros(total.shape, jnp.float32)
    acc[...] = jnp.zeros(acc.shape, jnp.float32)

    def step(at, carry):
        start = pl.multiple_of(at * KROWS, KROWS)
        place = lax.broadcasted_iota(jnp.int32, (rows, KROWS), 1) + start
        allowed = (place >= low) & (place < high)
        tiles = [kv_ref[pl.ds(start, KROWS), 2 * HD * t : 2 * HD * (t + 1)] for t in range(3)]
        for head in range(HEADS):
            scores = dot32(queries[head], tiles[KEY_TILE[head]], NT)
            scores = jnp.where(allowed, scores, -1e30)
            before = top[head]
            now = jnp.maximum(before, jnp.max(scores, axis=1, keepdims=True))
            expd = jnp.exp(scores - now[:, :1])
            fade = jnp.exp(before - now)
            top[head] = now
            total[head] = total[head] * fade + jnp.sum(expd, axis=1, keepdims=True)
            acc[head] = acc[head] * fade + dot32(expd.astype(jnp.bfloat16), tiles[VALUE_TILE[head]], NN)
        return carry

    lax.fori_loop(bounds[block, 0], bounds[block, 1], step, 0)
    lane = lax.broadcasted_iota(jnp.int32, (rows, 2 * HD), 1)
    heard = [acc[head] / total[head] for head in range(HEADS)]
    o_ref[:, : 2 * HD] = jnp.where(lane < HD, heard[0], heard[1])
    o_ref[:, 2 * HD :] = pltpu.roll(heard[2], HD, 1)[:, :HD]
    logs = [top[head] + jnp.log(total[head]) for head in range(HEADS)]
    columns = jnp.where(lane == 0, logs[0], jnp.where(lane == 1, logs[1], logs[2]))
    lse_ref[...] = jnp.transpose(columns)[:8, :]


def attend(queries, window, low, high, bounds):
    rows, span = queries.shape[0], window.shape[0]
    blocks = rows // QROWS
    return pl.pallas_call(
        attend_kernel,
        out_shape=(
            jax.ShapeDtypeStruct((rows, WIDE), jnp.float32),
            jax.ShapeDtypeStruct((8, rows), jnp.float32),
        ),
        grid_spec=pltpu.PrefetchScalarGridSpec(
            num_scalar_prefetch=1,
            grid=(blocks,),
            in_specs=[
                pl.BlockSpec((QROWS, WIDE), lambda i, b: (i, 0)),
                pl.BlockSpec((span, 2 * WIDE), lambda i, b: (0, 0)),
                pl.BlockSpec((QROWS, 1), lambda i, b: (i, 0)),
                pl.BlockSpec((QROWS, 1), lambda i, b: (i, 0)),
            ],
            out_specs=(
                pl.BlockSpec((QROWS, WIDE), lambda i, b: (i, 0)),
                pl.BlockSpec((8, QROWS), lambda i, b: (0, i)),
            ),
            scratch_shapes=[
                pltpu.VMEM((HEADS, QROWS, 2 * HD), jnp.float32),
                pltpu.VMEM((HEADS, QROWS, 2 * HD), jnp.float32),
                pltpu.VMEM((HEADS, QROWS, 2 * HD), jnp.float32),
            ],
        ),
        compiler_params=pltpu.CompilerParams(dimension_semantics=("arbitrary",)),
        cost_estimate=pl.CostEstimate(
            flops=4 * rows * 2000 * WIDE, bytes_accessed=span * WIDE * 4, transcendentals=rows * 2000 * 3
        ),
        name="attend",
    )(bounds, queries, window, low[:, None], high[:, None])


def attend_back_kernel(bounds, q_ref, kv_ref, o_ref, do_ref, lse_ref, range_ref, dq_ref, dkv_ref, grown, dq_acc):
    block = pl.program_id(0)
    rows = q_ref.shape[0]

    @pl.when(block == 0)
    def _():
        grown[...] = jnp.zeros(grown.shape, jnp.float32)

    queries = head_rows(q_ref[...])
    upstream = head_rows_up(do_ref[...])
    product = do_ref[...].astype(jnp.float32) * o_ref[...]
    lane = lax.broadcasted_iota(jnp.int32, (rows, 2 * HD), 1)
    parts = [jnp.sum(p, axis=1, keepdims=True) for p in head_rows(product)]
    columns = jnp.where(lane == 0, parts[0], jnp.where(lane == 1, parts[1], parts[2]))
    deltas = jnp.transpose(columns)[:8, :]
    low, high = range_ref[0:1, :], range_ref[1:2, :]
    dq_acc[...] = jnp.zeros(dq_acc.shape, jnp.float32)

    def step(at, carry):
        start = pl.multiple_of(at * KROWS, KROWS)
        here = pl.ds(start, KROWS)
        place = lax.broadcasted_iota(jnp.int32, (KROWS, rows), 0) + start
        allowed = (place >= low) & (place < high)
        tiles = [kv_ref[here, 2 * HD * t : 2 * HD * (t + 1)] for t in range(3)]
        for head in range(HEADS):
            kt, vt = KEY_TILE[head], VALUE_TILE[head]
            scores = dot32(tiles[kt], queries[head], NT)
            probs = jnp.where(allowed, jnp.exp(scores - lse_ref[head : head + 1, :]), 0.0)
            d_probs = dot32(tiles[vt], upstream[head], NT)
            d_scores = (probs * (d_probs - deltas[head : head + 1, :])).astype(jnp.bfloat16)
            grown[here, 2 * HD * vt : 2 * HD * (vt + 1)] += dot32(probs.astype(jnp.bfloat16), upstream[head], NN)
            grown[here, 2 * HD * kt : 2 * HD * (kt + 1)] += dot32(d_scores, queries[head], NN)
            dq_acc[head] += dot32(d_scores, tiles[kt], TN)
        return carry

    lax.fori_loop(bounds[block, 0], bounds[block, 1], step, 0)
    dq_ref[:, : 2 * HD] = jnp.where(lane < HD, dq_acc[0], dq_acc[1])
    dq_ref[:, 2 * HD :] = dq_acc[2][:, :HD]

    @pl.when(block == pl.num_programs(0) - 1)
    def _():
        dkv_ref[...] = grown[...].astype(jnp.bfloat16)


def attend_back(queries, window, heard, d_heard, lse, ranges, bounds):
    rows, span = queries.shape[0], window.shape[0]
    blocks = rows // QROWS
    return pl.pallas_call(
        attend_back_kernel,
        out_shape=(
            jax.ShapeDtypeStruct((rows, WIDE), jnp.float32),
            jax.ShapeDtypeStruct((span, 2 * WIDE), jnp.bfloat16),
        ),
        grid_spec=pltpu.PrefetchScalarGridSpec(
            num_scalar_prefetch=1,
            grid=(blocks,),
            in_specs=[
                pl.BlockSpec((QROWS, WIDE), lambda i, b: (i, 0)),
                pl.BlockSpec((span, 2 * WIDE), lambda i, b: (0, 0)),
                pl.BlockSpec((QROWS, WIDE), lambda i, b: (i, 0)),
                pl.BlockSpec((QROWS, WIDE), lambda i, b: (i, 0)),
                pl.BlockSpec((8, QROWS), lambda i, b: (0, i)),
                pl.BlockSpec((8, QROWS), lambda i, b: (0, i)),
            ],
            out_specs=(
                pl.BlockSpec((QROWS, WIDE), lambda i, b: (i, 0)),
                pl.BlockSpec((span, 2 * WIDE), lambda i, b: (0, 0)),
            ),
            scratch_shapes=[
                pltpu.VMEM((span, 2 * WIDE), jnp.float32),
                pltpu.VMEM((HEADS, QROWS, 2 * HD), jnp.float32),
            ],
        ),
        compiler_params=pltpu.CompilerParams(dimension_semantics=("arbitrary",)),
        cost_estimate=pl.CostEstimate(
            flops=10 * rows * 2000 * WIDE, bytes_accessed=span * WIDE * 12, transcendentals=rows * 2000 * 3
        ),
        name="attend_back",
    )(bounds, queries, window, heard, d_heard, lse, ranges)


class Plan:
    def __init__(self, groups, reps):
        self.groups, self.reps = groups, reps
        self.count = groups * reps
        self.outer = groups // (2 * SPLIT)
        self.sequences = self.count // SPLIT

    def split(self, flat):
        return flat // self.reps // 2 % SPLIT

    def sequence(self, flat):
        group, rep = flat // self.reps, flat % self.reps
        return (group // (2 * SPLIT) * self.reps + rep) * 2 + group % 2

    def device(self, sequence, split):
        core, rest = sequence % 2, sequence // 2
        rep, outer = rest % self.reps, rest // self.reps
        return ((outer * SPLIT + split) * 2 + core) * self.reps + rep

    def inward(self, value):
        return lax.ppermute(value, AXES, [(f, self.device(f // SPLIT, f % SPLIT)) for f in range(self.count)])

    def outward(self, value):
        return lax.ppermute(value, AXES, [(self.device(f // SPLIT, f % SPLIT), f) for f in range(self.count)])

    def across(self, value, mask):
        pairs = [(f, self.device(self.sequence(f), self.split(f) ^ mask)) for f in range(self.count)]
        return lax.ppermute(value, AXES, pairs)

    def along(self, value, steps):
        pairs = [
            (f, self.device(self.sequence(f) + steps, self.split(f)))
            for f in range(self.count)
            if 0 <= self.sequence(f) + steps < self.sequences
        ]
        return lax.ppermute(value, AXES, pairs)

    def beside(self, value, mask):
        pairs = []
        for f in range(self.count):
            group, rep = f // self.reps, f % self.reps
            outer, split, core = group // (2 * SPLIT), group // 2 % SPLIT, group % 2
            mate = (outer * 2 + core) ^ mask
            pairs.append((f, ((mate // 2 * SPLIT + split) * 2 + mate % 2) * self.reps + rep))
        return lax.ppermute(value, AXES, pairs)

    def least(self, value):
        bit = 1
        while bit < self.count:
            value = jnp.minimum(value, lax.ppermute(value, AXES, [(f, f ^ bit) for f in range(self.count)]))
            bit *= 2
        return value


def collect(plan, piece, split):
    rows = piece.shape[0]
    whole = jnp.zeros((SPLIT * rows,) + piece.shape[1:], piece.dtype)
    parts = [piece] + [plan.across(piece, mask) for mask in range(1, SPLIT)]
    for mask, part in enumerate(parts):
        whole = lax.dynamic_update_slice_in_dim(whole, part, (split ^ mask) * rows, 0)
    return whole


def deal(plan, whole, split):
    rows = whole.shape[0] // SPLIT
    own = lax.dynamic_slice_in_dim(whole, split * rows, rows, 0)
    return [own] + [
        plan.across(lax.dynamic_slice_in_dim(whole, (split ^ mask) * rows, rows, 0), mask) for mask in range(1, SPLIT)
    ]


def by_split(parts, split, axis):
    stacked = jnp.stack(parts)
    return jnp.concatenate(
        [lax.dynamic_index_in_dim(stacked, split ^ k, 0, keepdims=False) for k in range(SPLIT)], axis=axis
    )


def value_order(columns):
    return jnp.concatenate([columns[..., 2 * HD :], columns[..., : 2 * HD]], axis=-1)


def value_back(columns):
    return jnp.concatenate([columns[..., HD:], columns[..., :HD]], axis=-1)


def local(plan, *arguments):
    (tokens, segments, w_in, b_attn, w_out, w_up, b_up, w_down, b_down, gains, offsets, cotangent) = arguments
    rows, width = tokens.shape
    hidden = b_up.shape[1] * plan.groups
    reach = -(-(MAXLEN - 1 - SPLIT * rows) // KROWS) * KROWS
    block_rows = SPLIT * rows
    score_scale = HD ** (-0.5)
    flat = lax.axis_index("group") * plan.reps + lax.axis_index("rep")
    group = lax.axis_index("group")
    split = plan.split(flat)
    sequence = plan.sequence(flat)
    mate = group // (2 * SPLIT) * 2 + group % 2
    everything = rows * plan.count

    clips = everything // MAXLEN
    place = lax.iota(jnp.int32, rows) + flat * rows
    hits = segments[None, :] == lax.iota(jnp.int32, clips)[:, None]
    starts = jnp.min(jnp.where(hits, place[None, :], everything), axis=1)
    starts = jnp.pad(starts, (0, 128 - clips), constant_values=everything)[None, :]
    resid = plan.inward(tokens)
    starts = plan.least(starts)[0, :clips]
    own_place = lax.iota(jnp.int32, block_rows) + sequence * block_rows
    begun = jnp.where(starts[None, :] <= own_place[:, None], starts[None, :], -everything)
    begun = jnp.max(begun, axis=1)
    inside = own_place < begun + MAXLEN
    origin = sequence * block_rows - block_rows - reach
    low = jnp.where(inside, begun, own_place) - origin
    high = jnp.where(inside, begun + MAXLEN, own_place + 1) - origin
    first_block = jnp.min(low.reshape(-1, QROWS), axis=1) // KROWS
    last_block = (jnp.max(high.reshape(-1, QROWS), axis=1) + KROWS - 1) // KROWS
    bounds = jnp.stack([first_block, last_block], axis=1)
    ranges = jnp.pad(jnp.stack([low, high]), ((0, 6), (0, 0)))

    shard = w_in.shape[1]
    columns = w_in.reshape(LAYERS, shard, 3, SPLIT, WIDE)
    columns = jnp.stack([columns[:, :, 0], columns[:, :, 1], value_order(columns[:, :, 2])], axis=2)
    columns = columns.transpose(3, 0, 1, 2, 4).reshape(SPLIT, LAYERS * shard, 3 * WIDE)
    vectors = jnp.concatenate(
        [
            b_attn.reshape(LAYERS, -1),
            gains.reshape(LAYERS, -1),
            offsets.reshape(LAYERS, -1),
            b_up.reshape(LAYERS, -1),
            b_down.reshape(LAYERS, -1),
        ],
        axis=1,
    )
    each = vectors.shape[1]
    rows_of = -(-LAYERS * each // (3 * WIDE))
    flat_vectors = jnp.pad(vectors.reshape(-1), (0, rows_of * 3 * WIDE - LAYERS * each)).reshape(rows_of, 3 * WIDE)
    payload = jnp.concatenate([columns, jnp.broadcast_to(flat_vectors, (SPLIT,) + flat_vectors.shape)], axis=1)
    depth = payload.shape[1]
    arrived = jnp.stack(deal(plan, payload.reshape(SPLIT * depth, 3 * WIDE), split))
    mates = plan.groups // SPLIT
    arrived = jnp.stack([arrived] + [plan.beside(arrived, mask) for mask in range(1, mates)])
    pieces = []
    for member in range(plan.groups):
        member_split = member // 2 % SPLIT
        member_mate = member // (2 * SPLIT) * 2 + member % 2
        pieces.append(arrived[member_mate ^ mate, member_split ^ split])
    in_weights = jnp.concatenate(
        [piece[: LAYERS * shard].reshape(LAYERS, shard, 3 * WIDE) for piece in pieces], axis=1
    )
    vectors = jnp.stack(
        [piece[LAYERS * shard :].reshape(-1)[: LAYERS * each].reshape(LAYERS, each) for piece in pieces], axis=1
    ).astype(jnp.float32)

    def whole_vector(layer, start, size):
        return vectors[layer, :, start : start + size].reshape(-1)

    piece = width // plan.groups

    resid = resid.astype(jnp.float32)
    stored = []
    for layer in range(LAYERS):
        full_out = lax.all_gather(w_out[layer], "group", axis=0, tiled=True)
        full_up = lax.all_gather(w_up[layer], "group", axis=0, tiled=True)
        full_down = lax.all_gather(w_down[layer], "group", axis=0, tiled=True)
        bias = [whole_vector(layer, k * piece, piece) for k in range(3)]
        gain = [whole_vector(layer, (3 + k) * piece, piece) for k in range(2)]
        offset = [whole_vector(layer, (5 + k) * piece, piece) for k in range(2)]
        up_bias = whole_vector(layer, 7 * piece, hidden // plan.groups)
        down_bias = whole_vector(layer, 7 * piece + hidden // plan.groups, piece)
        query_bias = lax.dynamic_slice_in_dim(bias[0], split * WIDE, WIDE)
        value_bias = value_order(lax.dynamic_slice_in_dim(bias[1], split * WIDE, WIDE))

        normed, unit_first, inverse_first = layer_norm(resid, gain[0], offset[0])
        first = collect(plan, normed.astype(jnp.bfloat16), split)
        mixed = dot32(first, in_weights[layer], NN)
        queries = ((mixed[:, :WIDE] + query_bias) * score_scale).astype(jnp.bfloat16)
        add = jnp.concatenate([jnp.zeros((WIDE,), jnp.float32), value_bias])
        key_value = (mixed[:, WIDE:] + add).astype(jnp.bfloat16)
        window = jnp.concatenate(
            [
                plan.along(key_value[-reach:], 2),
                plan.along(key_value, 1),
                key_value,
                plan.along(key_value, -1),
                plan.along(key_value[:reach], -2),
            ],
            axis=0,
        )
        attended, lse = attend(queries, window, low, high, bounds)
        heard = by_split(deal(plan, attended.astype(jnp.bfloat16), split), split, 1)
        middle = resid + dot32(heard, full_out, NN) + bias[2]
        normed, unit_second, inverse_second = layer_norm(middle, gain[1], offset[1])
        second = normed.astype(jnp.bfloat16)
        pre_act = dot32(second, full_up, NN) + up_bias
        active = jax.nn.gelu(pre_act, approximate=False).astype(jnp.bfloat16)
        resid = middle + dot32(active, full_down, NN) + down_bias
        stored.append(
            (unit_first, inverse_first, first, queries, window, attended, lse, heard, unit_second, inverse_second)
            + (second, pre_act, active, full_out, full_up, full_down, gain)
        )
    output = plan.outward(resid.astype(jnp.bfloat16)).astype(jnp.float32)

    upstream = plan.inward(cotangent).astype(jnp.float32)
    shares = [None] * LAYERS
    small = [None] * LAYERS
    for layer in reversed(range(LAYERS)):
        (unit_first, inverse_first, first, queries, window, attended, lse, heard, unit_second, inverse_second) = stored[
            layer
        ][:10]
        second, pre_act, active, full_out, full_up, full_down, gain = stored[layer][10:]
        down_rounded = upstream.astype(jnp.bfloat16)
        g_down_b = jnp.sum(upstream, axis=0)
        g_down = dot32(active, down_rounded, TN).astype(jnp.bfloat16)
        d_pre = dot32(down_rounded, full_down, NT) * gelu_slope(pre_act)
        up_rounded = d_pre.astype(jnp.bfloat16)
        g_up_b = jnp.sum(d_pre, axis=0)
        g_up = dot32(second, up_rounded, TN).astype(jnp.bfloat16)
        d_second = dot32(up_rounded, full_up, NT)
        d_norm, g_gain_two, g_offset_two = norm_back(d_second, unit_second, inverse_second, gain[1])
        d_middle = upstream + d_norm
        middle_rounded = d_middle.astype(jnp.bfloat16)
        g_out_b = jnp.sum(d_middle, axis=0)
        g_out = dot32(heard, middle_rounded, TN).astype(jnp.bfloat16)
        d_heard = dot32(middle_rounded, full_out, NT).astype(jnp.bfloat16)
        by_head = d_heard.reshape(rows, SPLIT, WIDE).transpose(1, 0, 2).reshape(SPLIT * rows, WIDE)
        d_attended = by_split(deal(plan, by_head, split), split, 0)
        d_query, d_window = attend_back(queries, window, attended, d_attended, lse, ranges, bounds)
        d_own = d_window[reach + block_rows : reach + 2 * block_rows].astype(jnp.float32)
        d_own = d_own + plan.along(d_window[reach : reach + block_rows], -1).astype(jnp.float32)
        d_own = d_own + plan.along(d_window[reach + 2 * block_rows : reach + 3 * block_rows], 1).astype(jnp.float32)
        from_next = plan.along(d_window[:reach], -2).astype(jnp.float32)
        from_last = plan.along(d_window[reach + 3 * block_rows :], 2).astype(jnp.float32)
        d_own = d_own.at[block_rows - reach :].add(from_next).at[:reach].add(from_last)
        d_query = d_query * score_scale
        d_mixed = jnp.concatenate([d_query, d_own], axis=1)
        mixed_rounded = d_mixed.astype(jnp.bfloat16)
        sums = jnp.sum(d_mixed, axis=0)
        g_in = dot32(first, mixed_rounded, TN).astype(jnp.bfloat16)
        d_first_part = dot32(mixed_rounded, in_weights[layer], NT).astype(jnp.bfloat16)
        d_first = sum(part.astype(jnp.float32) for part in deal(plan, d_first_part, split))
        d_norm, g_gain_one, g_offset_one = norm_back(d_first, unit_first, inverse_first, gain[0])
        upstream = d_middle + d_norm

        came = lax.all_to_all(g_in.reshape(plan.groups, shard, 3 * WIDE), "group", 0, 0, tiled=True)
        came = came.reshape(plan.outer, SPLIT, 2, shard, 3, WIDE).astype(jnp.float32)
        came = jnp.sum(came, axis=(0, 2))
        came = jnp.stack([came[:, :, 0], came[:, :, 1], value_back(came[:, :, 2])], axis=2)
        g_in = came.transpose(1, 2, 0, 3).reshape(shard, 3 * width).astype(jnp.bfloat16)
        g_out = lax.psum_scatter(g_out, "group", scatter_dimension=0, tiled=True)
        g_up = lax.psum_scatter(g_up, "group", scatter_dimension=0, tiled=True)
        g_down = lax.psum_scatter(g_down, "group", scatter_dimension=0, tiled=True)
        shares[layer] = (g_in, g_out, g_up, g_down)
        blank = jnp.zeros((width,), jnp.float32)
        g_query_b = lax.dynamic_update_slice_in_dim(blank, sums[:WIDE], split * WIDE, 0)
        g_value_b = lax.dynamic_update_slice_in_dim(blank, value_back(sums[2 * WIDE :]), split * WIDE, 0)
        small[layer] = jnp.concatenate(
            [
                v.reshape(plan.groups, -1)
                for v in (
                    g_query_b,
                    g_value_b,
                    g_out_b,
                    g_gain_one,
                    g_gain_two,
                    g_offset_one,
                    g_offset_two,
                    g_up_b,
                    g_down_b,
                )
            ],
            axis=1,
        )
    input_grad = plan.outward(upstream.astype(jnp.bfloat16)).astype(jnp.float32)
    grads = []
    for field in range(4):
        grads.append(
            jnp.stack([lax.psum(shares[layer][field], "rep").astype(jnp.float32) for layer in range(LAYERS)])
        )
    small = lax.psum(jnp.stack(small, axis=1), AXES)
    small = lax.dynamic_index_in_dim(small, group, 0, keepdims=False)
    g_bias = small[:, : 3 * piece].reshape(LAYERS, 3, piece)
    g_gain = small[:, 3 * piece : 5 * piece].reshape(LAYERS, 2, piece)
    g_offset = small[:, 5 * piece : 7 * piece].reshape(LAYERS, 2, piece)
    g_up_b = small[:, 7 * piece : 7 * piece + hidden // plan.groups]
    g_down_b = small[:, 7 * piece + hidden // plan.groups :]
    return (
        output,
        input_grad,
        grads[0],
        g_bias,
        grads[1],
        grads[2],
        g_up_b,
        grads[3],
        g_down_b,
        g_gain,
        g_offset,
    )


def solution(mesh):
    both = P(AXES, None)
    in_specs = (
        both,
        P(AXES),
        P(None, "group", None),
        P(None, None, "group"),
        P(None, "group", None),
        P(None, "group", None),
        P(None, "group"),
        P(None, "group", None),
        P(None, "group"),
        P(None, None, "group"),
        P(None, None, "group"),
        both,
    )
    out_specs = (
        both,
        both,
        P(None, "group", None),
        P(None, None, "group"),
        P(None, "group", None),
        P(None, "group", None),
        P(None, "group"),
        P(None, "group", None),
        P(None, "group"),
        P(None, None, "group"),
        P(None, None, "group"),
    )
    plan = Plan(mesh.shape["group"], mesh.shape["rep"])
    return jax.shard_map(
        functools.partial(local, plan), mesh=mesh, in_specs=in_specs, out_specs=out_specs, check_vma=False
    )
```
